512 devices in a mesh: expert: 32 (over x, z_hi, core), tensor: 8 (over y), dp: 2 (over z_lo).
Axes of the slice: x: 4, y: 8, z: 8 (z_hi: 4, z_lo: 2; z = z_hi * 2 + z_lo), core: 2. Of those that a mesh axis runs over, the one named last changes fastest.
Arguments:
- tokens: bfloat16 [6144, 5120], P(('dp', 'expert'), 'tensor'), parts along dimension 0, may hold values from -6 to 6
- routes: int32 [6144, 6], P(('dp', 'expert')), parts along dimension 0, may hold values from 0 to 31, all different within a row; in each aligned block of 96 rows (0 to 95, 96 to 191, ...) at most 18 rows name the same one
- gates: float32 [6144, 6], P(('dp', 'expert')), parts along dimension 0, may hold values from 0.05 to 0.6
- gate_up: bfloat16 [32, 5120, 2, 1024], P('expert', None, None, 'tensor'), may hold values from -0.078125 to 0.078125
- down_weight: bfloat16 [32, 5120, 1024], P('expert', None, 'tensor'), may hold values from -0.1875 to 0.1875
- old_map: int32 [32], replicated, may hold values from 0 to 31, each once
- new_map: int32 [32], replicated, may hold values from 0 to 31, each once
Outputs:
- mixed: bfloat16 [6144, 5120], P(('dp', 'expert'), 'tensor'), parts along dimension 0
The draws below stay inside these ranges and needn't reach their ends.
There are 2 independent parts, one for each index of `dp`. The reference program is written for one: setup_inputs(seed, part) draws one part's arguments, and reference() takes and returns one part's arrays. A program takes and returns all parts, laid end to end along the dimension named above; an argument that names none is the same for every part. Nothing has to cross between parts.
Inputs may be any that keep to these rules, and one draw needn't show every extreme that they name: `routes`: each row names 6 different slots; in each aligned block of 96 rows (the rows of one index of expert) no slot is named by more than 18 rows; since each row names 6 different slots, every slot is then named by exactly 18 rows of every block. `old_map`: each expert appears exactly once. `new_map`: each expert appears exactly once.
All inputs are finite; a program needn't handle non-finite values.
Results may differ from the reference program's by a relative error of at most 0.0058.
Values may be sent and summed in bfloat16 or wider, within the bound.
No kernel may reach another device: no remote copies, remote signals or barrier semaphores. Data moves between devices by JAX's collectives and lax.ppermute only.
A program may use at most 64 MiB of HBM per device.

```python
import math
import jax
import jax.numpy as jnp
import numpy as np
from jax import lax

D = 5120
HID = 1024
TOP = 6
TOK_DEV = 96
EXPERTS = 32
CAP = 18
TOKENS = 3072
N_EXPERT = 32


def steps_of(key, shape, cuts, low, largest):
    level, own = 1.0, jax.random.fold_in(key, 6)
    for axis_at, parts in cuts:
        steps = jnp.exp(jax.random.uniform(jax.random.fold_in(own, axis_at), (parts,), jnp.float32, low / len(cuts), largest / len(cuts)))
        level = level * jnp.repeat(steps, shape[axis_at] // parts).reshape([-1 if axis == axis_at else 1 for axis in range(len(shape))])
    return level


def shared_out(own_key, own, number, rows, amount, top, most, lean):
    sequence = jax.random.permutation(own_key, amount)
    packed, ordinary = load_shares(amount, rows * top, most, lean, True), load_shares(amount, rows * top, most, lean, False)
    places = jnp.arange(amount)

    def named(sizes, turn):
        used = int((sizes > 0).sum())
        fixed = max(1, used // 4)
        shifted = fixed + (places - fixed + turn * (used - fixed)) % max(1, amount - fixed)
        return jnp.zeros((amount,), jnp.int32).at[sequence[jnp.where(places < fixed, places, shifted)]].set(jnp.asarray(sizes, jnp.int32))

    sizes = jnp.where(number % 4 == 0, named(packed, number // 4), named(ordinary, number - number // 4 - 1))
    mixed = jax.random.permutation(jax.random.fold_in(own, 3), amount)
    donor, sink = mixed[0:amount // 2 * 2:2], mixed[1:amount // 2 * 2:2]
    slack = jnp.minimum(sizes[donor] - 1, most - sizes[sink]) // 2
    slack = jnp.where((donor == sequence[0]) | (sink == sequence[0]) | (sizes[sink] == 0), 0, jnp.maximum(slack, 0))
    shifted = jax.random.randint(jax.random.fold_in(own, 4), (amount // 2,), 0, 1 << 20) % (slack + 1)
    sizes = sizes.at[donor].add(-shifted).at[sink].add(shifted)
    members = jnp.searchsorted(jnp.cumsum(sizes), jnp.arange(rows * top), side="right").astype(jnp.int32)
    listing = members.reshape(top, rows).T
    listing = listing[jax.random.permutation(jax.random.fold_in(own, 1), rows)]
    turn = jax.random.randint(jax.random.fold_in(own, 2), (rows, 1), 0, top)
    return jnp.take_along_axis(listing, (jnp.arange(top)[None, :] + turn) % top, axis=1)


def load_shares(amount, total, most, skew, full):
    loads = [(1 << 20) // math.isqrt(rank ** skew) + 1 for rank in range(1, amount + 1)]
    largest = most if full else min(most, max(-(-total // amount), total * loads[0] // sum(loads)))
    least = 1 if total - largest >= amount - 1 else 0
    holding, spare = [largest] + [least] * (amount - 1), total - largest - least * (amount - 1)
    while spare > 0:
        candidates = [i for i in range(1, amount) if holding[i] < largest] or [i for i in range(1, amount) if holding[i] < most]
        mass, budget = sum([loads[i] for i in candidates]), spare
        for i in candidates:
            more = min(most - holding[i], max(1, budget * loads[i] // mass), spare)
            holding[i] = holding[i] + more
            spare = spare - more
    return np.array(holding)


def gaussian(stream_key, extent, width, most, split=(), held_as=jnp.bfloat16):
    drawn = width * jax.random.normal(stream_key, extent, jnp.float32)
    if split:
        drawn = drawn * steps_of(stream_key, extent, split, -0.22, 0.18)
    return jnp.clip(drawn, -most, most).astype(held_as)


def setup_inputs(seed: int = 0, part: int = 0) -> dict:
    keys = jax.random.split(jax.random.key(seed), 8)
    part_keys = jax.random.split(jax.random.fold_in(keys[7], part), 8)
    tokens = gaussian(part_keys[0], (TOKENS, D), 1.0, 6.0, ((0, 32), (1, 8)))
    routes_keys = jax.random.split(jax.random.fold_in(part_keys[1], 1), TOKENS // TOK_DEV)
    routes_turns = jax.random.permutation(jax.random.fold_in(part_keys[1], 3), TOKENS // TOK_DEV)
    routes = jax.vmap(lambda own, number: shared_out(jax.random.fold_in(part_keys[1], 2), own, number, TOK_DEV, EXPERTS, TOP, CAP, 2))(routes_keys, routes_turns).reshape((TOKENS, TOP))
    gates = jnp.clip(0.05 + 0.55 * jax.random.uniform(part_keys[2], (TOKENS, TOP), jnp.float32) ** steps_of(part_keys[2], (TOKENS, TOP), ((0, 32),), -0.2, 0.2), 0.05, 0.6)
    gate_up = gaussian(keys[3], (EXPERTS, D, 2, HID), D ** -0.5, 0.078125, ((0, 32), (3, 8)))
    down_weight = gaussian(keys[4], (EXPERTS, D, HID), HID ** -0.5, 0.1875, ((0, 32), (2, 8)))
    old_map = jax.random.permutation(keys[5], EXPERTS).astype(jnp.int32)
    new_map = jax.random.permutation(keys[6], EXPERTS).astype(jnp.int32)
    return {"tokens": tokens, "routes": routes, "gates": gates, "gate_up": gate_up, "down_weight": down_weight, "old_map": old_map, "new_map": new_map}


def reference(tokens, routes, gates, gate_up, down_weight, old_map, new_map):
    slot_ids = jnp.arange(EXPERTS, dtype=jnp.int32)
    holder = jnp.sum(jnp.where(new_map[:, None] == old_map[None, :], slot_ids[None, :], 0), axis=1).astype(jnp.int32)
    buffer_rows = N_EXPERT * CAP

    def one_slot(carry, slot):
        chosen = routes == slot
        token_gate = jnp.sum(jnp.where(chosen, gates, 0.0), axis=1)
        picked = jnp.any(chosen, axis=1)
        order = jnp.argsort(jnp.where(picked, 0, 1).astype(jnp.int32), stable=True)[:buffer_rows]
        inputs = tokens[order]
        owner = holder[slot]
        weight_in = lax.dynamic_index_in_dim(gate_up, owner, 0, keepdims=False)
        weight_out = lax.dynamic_index_in_dim(down_weight, owner, 0, keepdims=False)
        gate = jnp.dot(inputs, weight_in[:, 0, :], preferred_element_type=jnp.float32)
        up = jnp.dot(inputs, weight_in[:, 1, :], preferred_element_type=jnp.float32)
        act = (jax.nn.silu(gate) * up).astype(jnp.bfloat16)
        expert_out = jnp.dot(act, weight_out.T, preferred_element_type=jnp.float32).astype(jnp.bfloat16)
        contribution = token_gate[order][:, None] * expert_out.astype(jnp.float32)
        return carry.at[order].add(contribution), None

    mixed, _ = lax.scan(one_slot, jnp.zeros((TOKENS, D), jnp.float32), slot_ids)
    return mixed.astype(jnp.bfloat16)
```

```python
import jax
import jax.numpy as jnp
from jax import lax
from jax.sharding import Mesh
from jax.sharding import PartitionSpec as P


EXPERT = ("expert_0", "expert_1", "expert_2")
CHIPS = ("expert_0", "expert_1")
DP_EXPERT = ("dp", "expert_0", "expert_1", "expert_2")


def dot(a, b, dims=((1,), (0,))):
    return lax.dot_general(a, b, (dims, ((), ())), preferred_element_type=jnp.float32)


def ring_pairs(size, step):
    return [(i, (i + step) % size) for i in range(size)]


def ring(x, size, use):
    forward = [(i, (i + 1) % size) for i in range(size)]
    backward = [(i, (i - 1) % size) for i in range(size)]
    rows = x.shape[0]
    use(x, 0, slice(0, rows))
    up = down = x
    for step in range(1, size // 2):
        up = lax.ppermute(up, "tensor", forward)
        down = lax.ppermute(down, "tensor", backward)
        use(up, -step, slice(0, rows))
        use(down, step, slice(0, rows))
    half = rows // 2
    use(lax.ppermute(up[:half], "tensor", forward), size // 2, slice(0, half))
    use(lax.ppermute(down[half:], "tensor", backward), size // 2, slice(half, rows))


def local(tokens, routes, gates, gate_up, down_weight, old_map, new_map):
    experts = lax.axis_size(EXPERT)
    chips = lax.axis_size(CHIPS)
    size = lax.axis_size("tensor")
    me = lax.axis_index("tensor")
    tok_rows, part = tokens.shape
    picks = routes.shape[1]
    capacity = (tok_rows * picks + experts - 1) // experts
    width = gate_up.shape[1]
    hidden = down_weight.shape[2]
    bf16 = jnp.bfloat16

    down_parts = down_weight.reshape(size, width // size, hidden)
    down_from = {}
    for step in (1, 7, 2, 6, 3, 5, 4):
        block = lax.dynamic_index_in_dim(down_parts, lax.rem(me + step, size), 0, keepdims=False)
        down_from[size - step] = lax.ppermute(block, "tensor", ring_pairs(size, step))
    down_from[0] = lax.dynamic_index_in_dim(down_parts, me, 0, keepdims=False)

    slot_ids = jnp.arange(experts, dtype=jnp.int32)
    holder = jnp.sum(jnp.where(new_map[:, None] == old_map[None, :], slot_ids[None, :], 0), axis=1)
    target = jnp.sum(
        jnp.where(routes[:, :, None] == slot_ids[None, None, :], holder[None, None, :], 0), axis=2
    )
    hits = target[:, :, None] == slot_ids[None, None, :]
    member = jnp.any(hits, axis=1)
    weight = jnp.sum(jnp.where(hits, gates[:, :, None], 0.0), axis=1)
    ones = jnp.tril(jnp.ones((tok_rows, tok_rows), bf16), -1)
    position = dot(ones, member.astype(bf16)).astype(jnp.int32)
    place = jnp.where(member, position, -1)
    cap_ids = jnp.arange(capacity, dtype=jnp.int32)
    order = jnp.arange(experts).reshape(chips, 2).T.reshape(-1)
    matches = place[:, order][:, :, None] == cap_ids[None, None, :]
    assign = matches.astype(bf16).reshape(tok_rows, experts * capacity)
    combine = jnp.where(matches, weight[:, order][:, :, None], 0.0).reshape(tok_rows, experts * capacity)
    outgoing = dot(assign, tokens, ((0,), (0,))).astype(bf16)

    weight_in = gate_up.reshape(size, part, 2 * hidden)

    def gathered(x):
        pieces = []

        def use(block, distance, rows_of):
            w = lax.dynamic_index_in_dim(weight_in, lax.rem(me + distance + size, size), 0, keepdims=False)
            pieces.append((dot(block, w), rows_of))

        ring(x, size, use)
        total = sum(p for p, s in pieces[:-2])
        total = total + jnp.concatenate([pieces[-2][0], pieces[-1][0]], axis=0)
        return (jax.nn.silu(total[:, :hidden]) * total[:, hidden:]).astype(bf16)

    def expert_rows(x):
        act = gathered(x)
        pieces = []

        def use(block, distance, rows_of):
            pieces.append((dot(block, down_from[distance % size], ((1,), (1,))), rows_of))

        ring(act, size, use)
        total = sum(p for p, s in pieces[:-2])
        total = total + jnp.concatenate([pieces[-2][0], pieces[-1][0]], axis=0)
        return total.astype(bf16)

    own_core = lax.axis_index("expert_2")
    both = outgoing.reshape(2, chips * capacity, part)
    mine = lax.dynamic_index_in_dim(both, own_core, 0, keepdims=False)
    other = lax.dynamic_index_in_dim(both, 1 - own_core, 0, keepdims=False)
    swap = [(0, 1), (1, 0)]
    other = lax.ppermute(other, "expert_2", swap)

    def over_chips(x):
        x = x.reshape(chips, capacity, part)
        x = lax.all_to_all(x, CHIPS, 0, 0, tiled=True)
        return x.reshape(chips * capacity, part)

    back_mine = over_chips(expert_rows(over_chips(mine)))
    back_other = over_chips(expert_rows(over_chips(other)))
    back_other = lax.ppermute(back_other, "expert_2", swap)
    combine = combine.reshape(tok_rows, 2, chips * capacity)
    take = lambda i: lax.dynamic_index_in_dim(combine, i, 1, keepdims=False)

    def mix(c, rows):
        return jnp.dot(
            c, rows.astype(jnp.float32), precision=lax.Precision.HIGHEST, preferred_element_type=jnp.float32
        )

    return (mix(take(own_core), back_mine) + mix(take(1 - own_core), back_other)).astype(bf16)


def solution(mesh):
    split = Mesh(
        mesh.devices.reshape(4, 4, 2, mesh.shape["tensor"], mesh.shape["dp"]),
        ("expert_0", "expert_1", "expert_2", "tensor", "dp"),
    )
    in_specs = (
        P(DP_EXPERT, "tensor"),
        P(DP_EXPERT, None),
        P(DP_EXPERT, None),
        P(EXPERT, None, None, "tensor"),
        P(EXPERT, None, "tensor"),
        P(),
        P(),
    )
    return jax.shard_map(local, mesh=split, in_specs=in_specs, out_specs=P(DP_EXPERT, "tensor"), check_vma=False)
```

```python
import jax
import jax.numpy as jnp
from jax import lax
from jax.sharding import Mesh
from jax.sharding import PartitionSpec as P


EXPERT = ("expert_0", "expert_1", "expert_2")
DP_EXPERT = ("dp", "expert_0", "expert_1", "expert_2")


def dot(a, b, dims=((1,), (0,))):
    return lax.dot_general(a, b, (dims, ((), ())), preferred_element_type=jnp.float32)


def shift(size, step):
    return [(i, (i + step) % size) for i in range(size)]


def ring(x, size, use):
    rows = x.shape[0]
    use(x, 0, 0)
    up = down = x
    for step in range(1, size // 2):
        up = lax.ppermute(up, "tensor", shift(size, 1))
        down = lax.ppermute(down, "tensor", shift(size, -1))
        use(up, -step, 0)
        use(down, step, 0)
    half = rows // 2
    use(lax.ppermute(up[:half], "tensor", shift(size, 1)), size // 2, 0)
    use(lax.ppermute(down[half:], "tensor", shift(size, -1)), size // 2, half)


def down_rows(down_weight, size, part, hidden):
    me, pair = lax.axis_index("tensor"), lax.axis_index("dp")
    blocks = down_weight.reshape(size, part, hidden)
    steps = ((1, 2, -3), (-1, -2, 3))
    got = []
    for first, second in zip(*steps):
        step = jnp.where(pair == 0, first, second)
        block = lax.dynamic_index_in_dim(blocks, lax.rem(me + step + size, size), 0, keepdims=False)
        perm = [(2 * i, 2 * ((i + first) % size)) for i in range(size)]
        perm += [(2 * i + 1, 2 * ((i + second) % size) + 1) for i in range(size)]
        got.append(lax.ppermute(block, ("tensor", "dp"), perm))
    half = part // 2
    far = lax.rem(me + size // 2, size)
    block = lax.dynamic_slice(blocks, (far, pair * half, 0), (1, half, hidden))[0]
    got.append(lax.ppermute(block, "tensor", shift(size, size // 2)))
    got = jnp.concatenate(got, axis=0)
    other = lax.ppermute(got, "dp", [(0, 1), (1, 0)])
    a = jnp.where(pair == 0, got, other)
    b = jnp.where(pair == 0, other, got)
    own = lax.dynamic_index_in_dim(blocks, me, 0, keepdims=False)
    piece = lambda x, i: x[i * part : (i + 1) * part]
    far = jnp.concatenate([a[3 * part :], b[3 * part :]], axis=0)
    near = [own, piece(b, 0), piece(b, 1), piece(a, 2), far, piece(b, 2), piece(a, 1), piece(a, 0)]
    twice = jnp.stack(near + near)
    return lax.dynamic_slice_in_dim(twice, lax.rem(size - me, size), size, 0)


def local(tokens, routes, gates, gate_up, down_weight, old_map, new_map):
    experts = lax.axis_size(EXPERT)
    size = lax.axis_size("tensor")
    me = lax.axis_index("tensor")
    tok_rows, part = tokens.shape
    picks = routes.shape[1]
    capacity = (tok_rows * picks + experts - 1) // experts
    hidden = down_weight.shape[2]
    rows = experts * capacity
    bf16 = jnp.bfloat16

    slot_ids = jnp.arange(experts, dtype=jnp.int32)
    holder = jnp.sum(jnp.where(new_map[:, None] == old_map[None, :], slot_ids[None, :], 0), axis=1)
    target = jnp.sum(
        jnp.where(routes[:, :, None] == slot_ids[None, None, :], holder[None, None, :], 0), axis=2
    )
    hits = target[:, :, None] == slot_ids[None, None, :]
    member = jnp.any(hits, axis=1)
    weight = jnp.sum(jnp.where(hits, gates[:, :, None], 0.0), axis=1)
    ones = jnp.tril(jnp.ones((tok_rows, tok_rows), bf16), -1)
    position = dot(ones, member.astype(bf16)).astype(jnp.int32)
    place = jnp.where(member, position, -1)
    cap_ids = jnp.arange(capacity, dtype=jnp.int32)
    matches = place[:, :, None] == cap_ids[None, None, :]
    assign = matches.astype(bf16).reshape(tok_rows, rows)
    combine = jnp.where(matches, weight[:, :, None], 0.0).reshape(tok_rows, rows)
    outgoing = dot(assign, tokens, ((0,), (0,))).astype(bf16)

    def exchange(x):
        x = x.reshape(experts, capacity // 2, 2, part)
        x = lax.all_to_all(x, EXPERT, 0, 0, tiled=True)
        return x.reshape(rows, part)

    arrived = exchange(outgoing)
    down_mine = down_rows(down_weight, size, part, hidden)

    weight_in = gate_up.reshape(size, part, 2 * hidden)

    def projected(x):
        pieces = []

        def use(block, distance, start):
            w = lax.dynamic_index_in_dim(weight_in, lax.rem(me + distance + size, size), 0, keepdims=False)
            pieces.append(dot(block, w))

        ring(x, size, use)
        total = sum(pieces[:-2]) + jnp.concatenate(pieces[-2:], axis=0)
        return (jax.nn.silu(total[:, :hidden]) * total[:, hidden:]).astype(bf16)

    half = rows // 2
    act_a, act_b = projected(arrived[:half]), projected(arrived[half:])
    all_a = lax.all_to_all(jnp.broadcast_to(act_a[None], (size, half, hidden)), "tensor", 0, 0, tiled=True)
    all_b = lax.all_gather(act_b, "tensor")

    def outputs(act):
        return dot(act, down_mine, ((0, 2), (0, 2))).astype(bf16)

    expert_out = jnp.concatenate([outputs(all_a), outputs(all_b)], axis=0)
    returned = exchange(expert_out)
    mixed = jnp.dot(
        combine,
        returned.astype(jnp.float32),
        precision=lax.Precision.HIGHEST,
        preferred_element_type=jnp.float32,
    )
    return mixed.astype(bf16)


def solution(mesh):
    split = Mesh(
        mesh.devices.reshape(4, 4, 2, mesh.shape["tensor"], mesh.shape["dp"]),
        ("expert_0", "expert_1", "expert_2", "tensor", "dp"),
    )
    in_specs = (
        P(DP_EXPERT, "tensor"),
        P(DP_EXPERT, None),
        P(DP_EXPERT, None),
        P(EXPERT, None, None, "tensor"),
        P(EXPERT, None, "tensor"),
        P(),
        P(),
    )
    return jax.shard_map(local, mesh=split, in_specs=in_specs, out_specs=P(DP_EXPERT, "tensor"), check_vma=False)
```

```python
import jax
import jax.numpy as jnp
from jax import lax
from jax.sharding import Mesh
from jax.sharding import PartitionSpec as P


EXPERT = ("expert_0", "expert_1", "expert_2")
DP_EXPERT = ("dp", "expert_0", "expert_1", "expert_2")


def dot(a, b, dims=((1,), (0,))):
    return lax.dot_general(a, b, (dims, ((), ())), preferred_element_type=jnp.float32)


def shift(size, step):
    return [(i, (i + step) % size) for i in range(size)]


def ring(x, size, last, use):
    use(x, 0)
    up = down = x
    for step in range(1, size // 2):
        up = lax.ppermute(up, "tensor", shift(size, 1))
        down = lax.ppermute(down, "tensor", shift(size, -1))
        use(up, -step)
        use(down, step)
    far = lax.ppermute(up if last > 0 else down, "tensor", shift(size, last))
    use(far, size // 2)


def down_rows(down_weight, size, part, hidden):
    pair = lax.axis_index("dp")
    half = part // 2
    blocks = down_weight.reshape(size, part, hidden)
    mine = lax.dynamic_slice_in_dim(blocks, pair * half, half, 1)
    mine = lax.all_to_all(mine, "tensor", 0, 0, tiled=True)
    other = lax.ppermute(mine, "dp", [(0, 1), (1, 0)])
    low = jnp.where(pair == 0, mine, other)
    high = jnp.where(pair == 0, other, mine)
    return jnp.concatenate([low, high], axis=1)


def local(tokens, routes, gates, gate_up, down_weight, old_map, new_map):
    experts = lax.axis_size(EXPERT)
    size = lax.axis_size("tensor")
    me = lax.axis_index("tensor")
    tok_rows, part = tokens.shape
    picks = routes.shape[1]
    capacity = (tok_rows * picks + experts - 1) // experts
    hidden = down_weight.shape[2]
    rows = experts * capacity
    bf16 = jnp.bfloat16

    slot_ids = jnp.arange(experts, dtype=jnp.int32)
    holder = jnp.sum(jnp.where(new_map[:, None] == old_map[None, :], slot_ids[None, :], 0), axis=1)
    target = jnp.sum(
        jnp.where(routes[:, :, None] == slot_ids[None, None, :], holder[None, None, :], 0), axis=2
    )
    hits = target[:, :, None] == slot_ids[None, None, :]
    member = jnp.any(hits, axis=1)
    weight = jnp.sum(jnp.where(hits, gates[:, :, None], 0.0), axis=1)
    ones = jnp.tril(jnp.ones((tok_rows, tok_rows), bf16), -1)
    position = dot(ones, member.astype(bf16)).astype(jnp.int32)
    place = jnp.where(member, position, -1)
    cap_ids = jnp.arange(capacity, dtype=jnp.int32)
    matches = place[:, :, None] == cap_ids[None, None, :]
    assign = matches.astype(bf16).reshape(tok_rows, rows)
    combine = jnp.where(matches, weight[:, :, None], 0.0).reshape(tok_rows, rows)
    outgoing = dot(assign, tokens, ((0,), (0,))).astype(bf16)

    def exchange(x):
        x = x.reshape(experts, capacity // 2, 2, part)
        x = lax.all_to_all(x, EXPERT, 0, 0, tiled=True)
        return x.reshape(rows, part)

    arrived = lax.optimization_barrier(exchange(outgoing))
    down_mine = down_rows(down_weight, size, part, hidden)

    weight_in = gate_up.reshape(size, part, 2 * hidden)

    def projected(x, last):
        pieces = []

        def use(block, distance):
            w = lax.dynamic_index_in_dim(weight_in, lax.rem(me + distance + size, size), 0, keepdims=False)
            pieces.append(dot(block, w))

        ring(x, size, last, use)
        total = sum(pieces)
        return (jax.nn.silu(total[:, :hidden]) * total[:, hidden:]).astype(bf16)

    half = rows // 2
    act_a, act_b = projected(arrived[:half], 1), projected(arrived[half:], -1)
    all_a = lax.all_to_all(jnp.broadcast_to(act_a[None], (size, half, hidden)), "tensor", 0, 0, tiled=True)
    all_b = lax.all_gather(act_b, "tensor")

    def outputs(act):
        return dot(act, down_mine, ((0, 2), (0, 2))).astype(bf16)

    expert_out = jnp.concatenate([outputs(all_a), outputs(all_b)], axis=0)
    returned = exchange(expert_out)
    mixed = jnp.dot(
        combine,
        returned.astype(jnp.float32),
        precision=lax.Precision.HIGHEST,
        preferred_element_type=jnp.float32,
    )
    return mixed.astype(bf16)


def solution(mesh):
    split = Mesh(
        mesh.devices.reshape(4, 4, 2, mesh.shape["tensor"], mesh.shape["dp"]),
        ("expert_0", "expert_1", "expert_2", "tensor", "dp"),
    )
    in_specs = (
        P(DP_EXPERT, "tensor"),
        P(DP_EXPERT, None),
        P(DP_EXPERT, None),
        P(EXPERT, None, None, "tensor"),
        P(EXPERT, None, "tensor"),
        P(),
        P(),
    )
    return jax.shard_map(local, mesh=split, in_specs=in_specs, out_specs=P(DP_EXPERT, "tensor"), check_vma=False)
```

```python
import functools

import jax
import jax.numpy as jnp
from jax import lax
from jax.experimental import pallas as pl
from jax.experimental.pallas import tpu as pltpu
from jax.sharding import Mesh
from jax.sharding import PartitionSpec as P


EXPERT = ("expert_0", "expert_1", "expert_2")
DP_EXPERT = ("dp", "expert_0", "expert_1", "expert_2")


def dot(a, b, dims=((1,), (0,))):
    return lax.dot_general(a, b, (dims, ((), ())), preferred_element_type=jnp.float32)


def shift(size, step):
    return [(i, (i + step) % size) for i in range(size)]


def ring(x, size, last, use):
    use(x, 0)
    up = down = x
    for step in range(1, size // 2):
        up = lax.ppermute(up, "tensor", shift(size, 1))
        down = lax.ppermute(down, "tensor", shift(size, -1))
        use(up, -step)
        use(down, step)
    far = lax.ppermute(up if last > 0 else down, "tensor", shift(size, last))
    use(far, size // 2)


def pack_kernel(first, second, third, fourth, out):
    rows = first.shape[0]
    for i, ref in enumerate((first, second, third)):
        out[i * rows : (i + 1) * rows, :] = ref[...]
    out[3 * rows :, :] = fourth[...]


def place_kernel(size, place, own, mine, other, out):
    rows = own.shape[0]
    me = place[0]

    def put(distance, value, start=0):
        at = lax.rem(me + distance, size)
        out[pl.ds(at, 1), start : start + value.shape[0], :] = value[None]

    def fill(a, b):
        put(1, b[0:rows, :])
        put(2, b[rows : 2 * rows, :])
        put(size - 3, b[2 * rows : 3 * rows, :])
        put(size - 1, a[0:rows, :])
        put(size - 2, a[rows : 2 * rows, :])
        put(3, a[2 * rows : 3 * rows, :])
        put(size // 2, a[3 * rows :, :])
        put(size // 2, b[3 * rows :, :], rows // 2)

    put(0, own[...])

    @pl.when(place[1] == 0)
    def _():
        fill(mine, other)

    @pl.when(place[1] == 1)
    def _():
        fill(other, mine)


def down_rows(down_weight, size, part, hidden):
    me, pair = lax.axis_index("tensor"), lax.axis_index("dp")
    blocks = down_weight.reshape(size, part, hidden)
    steps = ((1, 2, -3), (-1, -2, 3))
    got = []
    for first, second in zip(*steps):
        step = jnp.where(pair == 0, first, second)
        block = lax.dynamic_index_in_dim(blocks, lax.rem(me + step + size, size), 0, keepdims=False)
        perm = [(2 * i, 2 * ((i + first) % size)) for i in range(size)]
        perm += [(2 * i + 1, 2 * ((i + second) % size) + 1) for i in range(size)]
        got.append(lax.ppermute(block, ("tensor", "dp"), perm))
    half = part // 2
    far = lax.rem(me + size // 2, size)
    block = lax.dynamic_slice(blocks, (far, pair * half, 0), (1, half, hidden))[0]
    got.append(lax.ppermute(block, "tensor", shift(size, size // 2)))
    vmem = pl.BlockSpec(memory_space=pltpu.VMEM)
    mine = pl.pallas_call(
        pack_kernel,
        out_shape=jax.ShapeDtypeStruct((3 * part + half, hidden), blocks.dtype),
        in_specs=[vmem] * 4,
        out_specs=vmem,
        name="pack",
    )(*got)
    other = lax.ppermute(mine, "dp", [(0, 1), (1, 0)])
    own = lax.dynamic_index_in_dim(blocks, me, 0, keepdims=False)
    return pl.pallas_call(
        functools.partial(place_kernel, size),
        out_shape=jax.ShapeDtypeStruct(blocks.shape, blocks.dtype),
        in_specs=[pl.BlockSpec(memory_space=pltpu.SMEM)] + [vmem] * 3,
        out_specs=vmem,
        name="place",
    )(jnp.stack([me, pair]).astype(jnp.int32), own, mine, other)


def local(tokens, routes, gates, gate_up, down_weight, old_map, new_map):
    experts = lax.axis_size(EXPERT)
    size = lax.axis_size("tensor")
    me = lax.axis_index("tensor")
    tok_rows, part = tokens.shape
    picks = routes.shape[1]
    capacity = (tok_rows * picks + experts - 1) // experts
    hidden = down_weight.shape[2]
    rows = experts * capacity
    bf16 = jnp.bfloat16

    slot_ids = jnp.arange(experts, dtype=jnp.int32)
    holder = jnp.sum(jnp.where(new_map[:, None] == old_map[None, :], slot_ids[None, :], 0), axis=1)
    target = jnp.sum(
        jnp.where(routes[:, :, None] == slot_ids[None, None, :], holder[None, None, :], 0), axis=2
    )
    hits = target[:, :, None] == slot_ids[None, None, :]
    member = jnp.any(hits, axis=1)
    weight = jnp.sum(jnp.where(hits, gates[:, :, None], 0.0), axis=1)
    ones = jnp.tril(jnp.ones((tok_rows, tok_rows), bf16), -1)
    position = dot(ones, member.astype(bf16)).astype(jnp.int32)
    place = jnp.where(member, position, -1)
    cap_ids = jnp.arange(capacity, dtype=jnp.int32)
    matches = place[:, :, None] == cap_ids[None, None, :]
    assign = matches.astype(bf16).reshape(tok_rows, rows)
    combine = jnp.where(matches, weight[:, :, None], 0.0).reshape(tok_rows, rows)
    outgoing = dot(assign, tokens, ((0,), (0,))).astype(bf16)

    def exchange(x):
        x = x.reshape(experts, capacity // 2, 2, part)
        x = lax.all_to_all(x, EXPERT, 0, 0, tiled=True)
        return x.reshape(rows, part)

    arrived = lax.optimization_barrier(exchange(outgoing))
    down_mine = down_rows(down_weight, size, part, hidden)

    weight_in = gate_up.reshape(size, part, 2, hidden)

    def projected(x, last):
        pieces = []

        def use(block, distance):
            w = lax.dynamic_index_in_dim(weight_in, lax.rem(me + distance + size, size), 0, keepdims=False)
            pieces.append(dot(block, w.reshape(part, 2 * hidden)))

        ring(x, size, last, use)
        total = sum(pieces)
        return (jax.nn.silu(total[:, :hidden]) * total[:, hidden:]).astype(bf16)

    half = rows // 2
    act_a, act_b = projected(arrived[:half], 1), projected(arrived[half:], -1)
    all_a = lax.all_to_all(jnp.broadcast_to(act_a[None], (size, half, hidden)), "tensor", 0, 0, tiled=True)
    all_b = lax.all_gather(act_b, "tensor")

    def outputs(act):
        return dot(act, down_mine, ((0, 2), (0, 2))).astype(bf16)

    expert_out = jnp.concatenate([outputs(all_a), outputs(all_b)], axis=0)
    returned = exchange(expert_out)
    mixed = jnp.dot(
        combine,
        returned.astype(jnp.float32),
        precision=lax.Precision.HIGHEST,
        preferred_element_type=jnp.float32,
    )
    return mixed.astype(bf16)


def solution(mesh):
    split = Mesh(
        mesh.devices.reshape(4, 4, 2, mesh.shape["tensor"], mesh.shape["dp"]),
        ("expert_0", "expert_1", "expert_2", "tensor", "dp"),
    )
    in_specs = (
        P(DP_EXPERT, "tensor"),
        P(DP_EXPERT, None),
        P(DP_EXPERT, None),
        P(EXPERT, None, None, "tensor"),
        P(EXPERT, None, "tensor"),
        P(),
        P(),
    )
    return jax.shard_map(local, mesh=split, in_specs=in_specs, out_specs=P(DP_EXPERT, "tensor"), check_vma=False)
```

```python
import functools

import jax
import jax.numpy as jnp
from jax import lax
from jax.experimental import pallas as pl
from jax.experimental.pallas import tpu as pltpu
from jax.sharding import Mesh
from jax.sharding import PartitionSpec as P


EXPERT = ("expert_0", "expert_1", "expert_2")
DP_EXPERT = ("dp", "expert_0", "expert_1", "expert_2")


def dot(a, b, dims=((1,), (0,))):
    return lax.dot_general(a, b, (dims, ((), ())), preferred_element_type=jnp.float32)


def shift(size, step):
    return [(i, (i + step) % size) for i in range(size)]


def hops(x, size, last):
    found = [(0, x)]
    up = down = x
    for step in range(1, size // 2):
        up = lax.ppermute(up, "tensor", shift(size, 1))
        down = lax.ppermute(down, "tensor", shift(size, -1))
        found += [(-step, up), (step, down)]
    found.append((size // 2, lax.ppermute(up if last > 0 else down, "tensor", shift(size, last))))
    return found


def product_of(me, size, distances, blocks, weight):
    return sum(
        jnp.dot(x[...], weight[lax.rem(me + d + size, size)], preferred_element_type=jnp.float32)
        for d, x in zip(distances, blocks)
    )


def first_kernel(size, distances, place, weight, *refs):
    count = len(distances)
    for chain in range(2):
        blocks = refs[chain * count : (chain + 1) * count]
        refs[2 * count + chain][...] = product_of(place[0], size, distances, blocks, weight)


def last_kernel(size, distances, place, weight, begun, *refs):
    *blocks, out = refs
    total = begun[...] + product_of(place[0], size, distances, blocks, weight)
    gate, up = total[:, : total.shape[1] // 2], total[:, total.shape[1] // 2 :]
    out[...] = (gate / (1.0 + jnp.exp(-gate)) * up).astype(out.dtype)


def pack_kernel(first, second, third, fourth, out):
    rows = first.shape[0]
    for i, ref in enumerate((first, second, third)):
        out[i * rows : (i + 1) * rows, :] = ref[...]
    out[3 * rows :, :] = fourth[...]


def place_kernel(size, place, own, mine, other, out):
    rows = own.shape[0]
    me = place[0]

    def put(distance, value, start=0):
        at = lax.rem(me + distance, size)
        out[pl.ds(at, 1), start : start + value.shape[0], :] = value[None]

    def fill(a, b):
        put(1, b[0:rows, :])
        put(2, b[rows : 2 * rows, :])
        put(size - 3, b[2 * rows : 3 * rows, :])
        put(size - 1, a[0:rows, :])
        put(size - 2, a[rows : 2 * rows, :])
        put(3, a[2 * rows : 3 * rows, :])
        put(size // 2, a[3 * rows :, :])
        put(size // 2, b[3 * rows :, :], rows // 2)

    put(0, own[...])

    @pl.when(place[1] == 0)
    def _():
        fill(mine, other)

    @pl.when(place[1] == 1)
    def _():
        fill(other, mine)


def down_rows(down_weight, after, place, size, part, hidden):
    me, pair = lax.axis_index("tensor"), lax.axis_index("dp")
    blocks = down_weight.reshape(size, part, hidden)
    steps = ((1, 2, -3), (-1, -2, 3))
    got = []
    for first, second in zip(*steps):
        step = jnp.where(pair == 0, first, second)
        block = lax.dynamic_index_in_dim(blocks, lax.rem(me + step + size, size), 0, keepdims=False)
        perm = [(2 * i, 2 * ((i + first) % size)) for i in range(size)]
        perm += [(2 * i + 1, 2 * ((i + second) % size) + 1) for i in range(size)]
        got.append(lax.ppermute(block, ("tensor", "dp"), perm))
    half = part // 2
    far = lax.rem(me + size // 2, size)
    block = lax.dynamic_slice(blocks, (far, pair * half, 0), (1, half, hidden))[0]
    got.append(lax.ppermute(block, "tensor", shift(size, size // 2)))
    vmem = pl.BlockSpec(memory_space=pltpu.VMEM)
    mine = pl.pallas_call(
        pack_kernel,
        out_shape=jax.ShapeDtypeStruct((3 * part + half, hidden), blocks.dtype),
        in_specs=[vmem] * 4,
        out_specs=vmem,
        name="pack",
    )(*got)
    mine, after = lax.optimization_barrier((mine, after))
    other = lax.ppermute(mine, "dp", [(0, 1), (1, 0)])
    own = lax.dynamic_index_in_dim(blocks, me, 0, keepdims=False)
    placed = pl.pallas_call(
        functools.partial(place_kernel, size),
        out_shape=jax.ShapeDtypeStruct(blocks.shape, blocks.dtype),
        in_specs=[pl.BlockSpec(memory_space=pltpu.SMEM)] + [vmem] * 3,
        out_specs=vmem,
        name="place",
    )(place, own, mine, other)
    return placed, after


def local(tokens, routes, gates, gate_up, down_weight, old_map, new_map):
    experts = lax.axis_size(EXPERT)
    size = lax.axis_size("tensor")
    me = lax.axis_index("tensor")
    tok_rows, part = tokens.shape
    picks = routes.shape[1]
    capacity = (tok_rows * picks + experts - 1) // experts
    hidden = down_weight.shape[2]
    rows = experts * capacity
    bf16 = jnp.bfloat16

    slot_ids = jnp.arange(experts, dtype=jnp.int32)
    holder = jnp.sum(jnp.where(new_map[:, None] == old_map[None, :], slot_ids[None, :], 0), axis=1)
    target = jnp.sum(
        jnp.where(routes[:, :, None] == slot_ids[None, None, :], holder[None, None, :], 0), axis=2
    )
    hits = target[:, :, None] == slot_ids[None, None, :]
    member = jnp.any(hits, axis=1)
    weight = jnp.sum(jnp.where(hits, gates[:, :, None], 0.0), axis=1)
    ones = jnp.tril(jnp.ones((tok_rows, tok_rows), bf16), -1)
    position = dot(ones, member.astype(bf16)).astype(jnp.int32)
    place = jnp.where(member, position, -1)
    cap_ids = jnp.arange(capacity, dtype=jnp.int32)
    matches = place[:, :, None] == cap_ids[None, None, :]
    assign = matches.astype(bf16).reshape(tok_rows, rows)
    combine = jnp.where(matches, weight[:, :, None], 0.0).reshape(tok_rows, rows)
    outgoing = dot(assign, tokens, ((0,), (0,))).astype(bf16)

    def exchange(x):
        x = x.reshape(experts, capacity // 2, 2, part)
        x = lax.all_to_all(x, EXPERT, 0, 0, tiled=True)
        return x.reshape(rows, part)

    arrived = lax.optimization_barrier(exchange(outgoing))
    place = jnp.stack([me, lax.axis_index("dp")]).astype(jnp.int32)
    down_mine, weight_in = down_rows(down_weight, gate_up, place, size, part, hidden)

    chains = [hops(arrived[: rows // 2], size, 1), hops(arrived[rows // 2 :], size, -1)]
    weight_in = weight_in.reshape(size, part, 2 * hidden)
    early = 5
    smem, vmem = pl.BlockSpec(memory_space=pltpu.SMEM), pl.BlockSpec(memory_space=pltpu.VMEM)
    begun = pl.pallas_call(
        functools.partial(first_kernel, size, [d for d, _ in chains[0][:early]]),
        out_shape=[jax.ShapeDtypeStruct((rows // 2, 2 * hidden), jnp.float32)] * 2,
        in_specs=[smem] + [vmem] * (1 + 2 * early),
        out_specs=[vmem] * 2,
        name="first",
    )(place, weight_in, *(x for chain in chains for _, x in chain[:early]))

    def finished(chain, total):
        return pl.pallas_call(
            functools.partial(last_kernel, size, [d for d, _ in chain[early:]]),
            out_shape=jax.ShapeDtypeStruct((rows // 2, hidden), bf16),
            in_specs=[smem] + [vmem] * (2 + len(chain) - early),
            out_specs=vmem,
            name="last",
        )(place, weight_in, total, *(x for _, x in chain[early:]))

    act_a, act_b = finished(chains[0], begun[0]), finished(chains[1], begun[1])
    some = 136
    all_a = lax.all_to_all(jnp.broadcast_to(act_a[None, :some], (size, some, hidden)), "tensor", 0, 0, tiled=True)
    all_b = lax.all_gather(jnp.concatenate([act_a[some:], act_b], axis=0), "tensor")

    def outputs(act):
        return dot(act, down_mine, ((0, 2), (0, 2))).astype(bf16)

    expert_out = jnp.concatenate([outputs(all_a), outputs(all_b)], axis=0)
    returned = exchange(expert_out)
    mixed = jnp.dot(
        combine,
        returned.astype(jnp.float32),
        precision=lax.Precision.HIGHEST,
        preferred_element_type=jnp.float32,
    )
    return mixed.astype(bf16)


def solution(mesh):
    split = Mesh(
        mesh.devices.reshape(4, 4, 2, mesh.shape["tensor"], mesh.shape["dp"]),
        ("expert_0", "expert_1", "expert_2", "tensor", "dp"),
    )
    in_specs = (
        P(DP_EXPERT, "tensor"),
        P(DP_EXPERT, None),
        P(DP_EXPERT, None),
        P(EXPERT, None, None, "tensor"),
        P(EXPERT, None, "tensor"),
        P(),
        P(),
    )
    return jax.shard_map(local, mesh=split, in_specs=in_specs, out_specs=P(DP_EXPERT, "tensor"), check_vma=False)
```

```python
import functools

import jax
import jax.numpy as jnp
from jax import lax
from jax.experimental import pallas as pl
from jax.experimental.pallas import tpu as pltpu
from jax.sharding import Mesh
from jax.sharding import PartitionSpec as P


EXPERT = ("expert_0", "expert_1", "expert_2")
SMALL = pltpu.CompilerParams(vmem_limit_bytes=12 * 1024 * 1024)
DP_EXPERT = ("dp", "expert_0", "expert_1", "expert_2")


def dot(a, b, dims=((1,), (0,))):
    return lax.dot_general(a, b, (dims, ((), ())), preferred_element_type=jnp.float32)


def shift(size, step):
    return [(i, (i + step) % size) for i in range(size)]


def hops(x, size, last):
    found = [(0, x)]
    up = down = x
    for step in range(1, size // 2):
        up = lax.ppermute(up, "tensor", shift(size, 1))
        down = lax.ppermute(down, "tensor", shift(size, -1))
        found += [(-step, up), (step, down)]
    found.append((size // 2, lax.ppermute(up if last > 0 else down, "tensor", shift(size, last))))
    return found


def product_of(me, size, distances, blocks, weight):
    return sum(
        jnp.dot(x[...], weight[lax.rem(me + d + size, size)], preferred_element_type=jnp.float32)
        for d, x in zip(distances, blocks)
    )


def first_kernel(size, distances, place, weight, *refs):
    count = len(distances)
    for chain in range(2):
        blocks = refs[chain * count : (chain + 1) * count]
        refs[2 * count + chain][...] = product_of(place[0], size, distances, blocks, weight)


def activation(size, distances, place, weight, begun, blocks):
    total = begun[...] + product_of(place[0], size, distances, blocks, weight)
    gate, up = total[:, : total.shape[1] // 2], total[:, total.shape[1] // 2 :]
    return (gate / (1.0 + jnp.exp(-gate)) * up).astype(jnp.bfloat16)


def last_a_kernel(size, distances, place, weight, begun, *refs):
    *blocks, spread, rest = refs
    act = activation(size, distances, place, weight, begun, blocks)
    some = spread.shape[1]
    for i in range(size):
        spread[i] = act[:some, :]
    rest[...] = act[some:, :]


def last_b_kernel(size, distances, place, weight, begun, *refs):
    *blocks, rest, out = refs
    out[: rest.shape[0], :] = rest[...]
    out[rest.shape[0] :, :] = activation(size, distances, place, weight, begun, blocks)


def pack_kernel(first, second, third, fourth, out):
    rows = first.shape[0]
    for i, ref in enumerate((first, second, third)):
        out[i * rows : (i + 1) * rows, :] = ref[...]
    out[3 * rows :, :] = fourth[...]


def place_kernel(size, place, own, mine, other, out):
    rows = own.shape[0]
    me = place[0]

    def put(distance, value, start=0):
        at = lax.rem(me + distance, size)
        out[pl.ds(at, 1), start : start + value.shape[0], :] = value[None]

    def fill(a, b):
        put(1, b[0:rows, :])
        put(2, b[rows : 2 * rows, :])
        put(size - 3, b[2 * rows : 3 * rows, :])
        put(size - 1, a[0:rows, :])
        put(size - 2, a[rows : 2 * rows, :])
        put(3, a[2 * rows : 3 * rows, :])
        put(size // 2, a[3 * rows :, :])
        put(size // 2, b[3 * rows :, :], rows // 2)

    put(0, own[...])

    @pl.when(place[1] == 0)
    def _():
        fill(mine, other)

    @pl.when(place[1] == 1)
    def _():
        fill(other, mine)


def down_rows(down_weight, after, place, size, part, hidden):
    me, pair = lax.axis_index("tensor"), lax.axis_index("dp")
    blocks = down_weight.reshape(size, part, hidden)
    steps = ((1, 2, -3), (-1, -2, 3))
    got = []
    for first, second in zip(*steps):
        step = jnp.where(pair == 0, first, second)
        block = lax.dynamic_index_in_dim(blocks, lax.rem(me + step + size, size), 0, keepdims=False)
        perm = [(2 * i, 2 * ((i + first) % size)) for i in range(size)]
        perm += [(2 * i + 1, 2 * ((i + second) % size) + 1) for i in range(size)]
        got.append(lax.ppermute(block, ("tensor", "dp"), perm))
    half = part // 2
    far = lax.rem(me + size // 2, size)
    block = lax.dynamic_slice(blocks, (far, pair * half, 0), (1, half, hidden))[0]
    got.append(lax.ppermute(block, "tensor", shift(size, size // 2)))
    vmem = pl.BlockSpec(memory_space=pltpu.VMEM)
    mine = pl.pallas_call(
        pack_kernel,
        out_shape=jax.ShapeDtypeStruct((3 * part + half, hidden), blocks.dtype),
        in_specs=[vmem] * 4,
        out_specs=vmem,
        name="pack",
        compiler_params=SMALL,
    )(*got)
    other = lax.ppermute(mine, "dp", [(0, 1), (1, 0)])
    own = lax.dynamic_index_in_dim(blocks, me, 0, keepdims=False)
    placed = pl.pallas_call(
        functools.partial(place_kernel, size),
        out_shape=jax.ShapeDtypeStruct(blocks.shape, blocks.dtype),
        in_specs=[pl.BlockSpec(memory_space=pltpu.SMEM)] + [vmem] * 3,
        out_specs=vmem,
        name="place",
        compiler_params=SMALL,
    )(place, own, mine, other)
    return placed, after


def local(tokens, routes, gates, gate_up, down_weight, old_map, new_map):
    experts = lax.axis_size(EXPERT)
    size = lax.axis_size("tensor")
    me = lax.axis_index("tensor")
    tok_rows, part = tokens.shape
    picks = routes.shape[1]
    capacity = (tok_rows * picks + experts - 1) // experts
    hidden = down_weight.shape[2]
    rows = experts * capacity
    bf16 = jnp.bfloat16

    slot_ids = jnp.arange(experts, dtype=jnp.int32)
    holder = jnp.sum(jnp.where(new_map[:, None] == old_map[None, :], slot_ids[None, :], 0), axis=1)
    target = jnp.sum(
        jnp.where(routes[:, :, None] == slot_ids[None, None, :], holder[None, None, :], 0), axis=2
    )
    hits = target[:, :, None] == slot_ids[None, None, :]
    member = jnp.any(hits, axis=1)
    weight = jnp.sum(jnp.where(hits, gates[:, :, None], 0.0), axis=1)
    ones = jnp.tril(jnp.ones((tok_rows, tok_rows), bf16), -1)
    position = dot(ones, member.astype(bf16)).astype(jnp.int32)
    place = jnp.where(member, position, -1)
    cap_ids = jnp.arange(capacity, dtype=jnp.int32)
    matches = place[:, :, None] == cap_ids[None, None, :]
    assign = matches.astype(bf16).reshape(tok_rows, rows)
    combine = jnp.where(matches, weight[:, :, None], 0.0).reshape(tok_rows, rows)
    outgoing = dot(assign, tokens, ((0,), (0,))).astype(bf16)

    def exchange(x):
        x = x.reshape(experts, capacity // 2, 2, part)
        x = lax.all_to_all(x, EXPERT, 0, 0, tiled=True)
        return x.reshape(rows, part)

    arrived = lax.optimization_barrier(exchange(outgoing))
    place = jnp.stack([me, lax.axis_index("dp")]).astype(jnp.int32)
    down_mine, weight_in = down_rows(down_weight, gate_up, place, size, part, hidden)

    chains = [hops(arrived[: rows // 2], size, 1), hops(arrived[rows // 2 :], size, -1)]
    weight_in = weight_in.reshape(size, part, 2 * hidden)
    early = 5
    smem, vmem = pl.BlockSpec(memory_space=pltpu.SMEM), pl.BlockSpec(memory_space=pltpu.VMEM)
    begun = pl.pallas_call(
        functools.partial(first_kernel, size, [d for d, _ in chains[0][:early]]),
        out_shape=[jax.ShapeDtypeStruct((rows // 2, 2 * hidden), jnp.float32)] * 2,
        in_specs=[smem] + [vmem] * (1 + 2 * early),
        out_specs=[vmem] * 2,
        name="first",
        compiler_params=SMALL,
    )(place, weight_in, *(x for chain in chains for _, x in chain[:early]))

    some = 136
    distances = [d for d, _ in chains[0][early:]]
    late = [smem] + [vmem] * (2 + len(distances))
    spread, rest = pl.pallas_call(
        functools.partial(last_a_kernel, size, distances),
        out_shape=[
            jax.ShapeDtypeStruct((size, some, hidden), bf16),
            jax.ShapeDtypeStruct((rows // 2 - some, hidden), bf16),
        ],
        in_specs=late,
        out_specs=[vmem] * 2,
        name="last_a",
        compiler_params=SMALL,
    )(place, weight_in, begun[0], *(x for _, x in chains[0][early:]))
    all_a = lax.all_to_all(spread, "tensor", 0, 0, tiled=True)
    act_b = pl.pallas_call(
        functools.partial(last_b_kernel, size, distances),
        out_shape=jax.ShapeDtypeStruct((rows - some, hidden), bf16),
        in_specs=late + [vmem],
        out_specs=vmem,
        name="last_b",
        compiler_params=SMALL,
    )(place, weight_in, begun[1], *(x for _, x in chains[1][early:]), rest)
    all_b = lax.all_gather(act_b, "tensor")

    def outputs(act):
        return dot(act, down_mine, ((0, 2), (0, 2))).astype(bf16)

    expert_out = jnp.concatenate([outputs(all_a), outputs(all_b)], axis=0)
    returned = exchange(expert_out)
    mixed = jnp.dot(
        combine,
        returned.astype(jnp.float32),
        precision=lax.Precision.HIGHEST,
        preferred_element_type=jnp.float32,
    )
    return mixed.astype(bf16)


def solution(mesh):
    split = Mesh(
        mesh.devices.reshape(4, 4, 2, mesh.shape["tensor"], mesh.shape["dp"]),
        ("expert_0", "expert_1", "expert_2", "tensor", "dp"),
    )
    in_specs = (
        P(DP_EXPERT, "tensor"),
        P(DP_EXPERT, None),
        P(DP_EXPERT, None),
        P(EXPERT, None, None, "tensor"),
        P(EXPERT, None, "tensor"),
        P(),
        P(),
    )
    return jax.shard_map(local, mesh=split, in_specs=in_specs, out_specs=P(DP_EXPERT, "tensor"), check_vma=False)
```

```python
import functools

import jax
import jax.numpy as jnp
from jax import lax
from jax.experimental import pallas as pl
from jax.experimental.pallas import tpu as pltpu
from jax.sharding import Mesh
from jax.sharding import PartitionSpec as P


EXPERT = ("expert_0", "expert_1", "expert_2")
SMALL = pltpu.CompilerParams(vmem_limit_bytes=12 * 1024 * 1024)
DP_EXPERT = ("dp", "expert_0", "expert_1", "expert_2")


def dot(a, b, dims=((1,), (0,))):
    return lax.dot_general(a, b, (dims, ((), ())), preferred_element_type=jnp.float32)


def shift(size, step):
    return [(i, (i + step) % size) for i in range(size)]


def hops(x, size, last):
    found = [(0, x)]
    up = down = x
    for step in range(1, size // 2):
        up = lax.ppermute(up, "tensor", shift(size, 1))
        down = lax.ppermute(down, "tensor", shift(size, -1))
        found += [(-step, up), (step, down)]
    found.append((size // 2, lax.ppermute(up if last > 0 else down, "tensor", shift(size, last))))
    return found


def relayout_kernel(x, out):
    out[0] = x[0].reshape(out.shape[1:])


def product_of(me, size, distances, blocks, weight):
    return sum(
        jnp.dot(x[...], weight[lax.rem(me + d + size, size)], preferred_element_type=jnp.float32)
        for d, x in zip(distances, blocks)
    )


def first_kernel(size, distances, place, weight, *refs):
    count = len(distances)
    for chain in range(2):
        blocks = refs[chain * count : (chain + 1) * count]
        refs[2 * count + chain][...] = product_of(place[0], size, distances, blocks, weight)


def activation(size, distances, place, weight, begun, blocks):
    total = begun[...] + product_of(place[0], size, distances, blocks, weight)
    gate, up = total[:, : total.shape[1] // 2], total[:, total.shape[1] // 2 :]
    return (gate / (1.0 + jnp.exp(-gate)) * up).astype(jnp.bfloat16)


def last_a_kernel(size, distances, place, weight, begun, *refs):
    *blocks, spread, rest = refs
    act = activation(size, distances, place, weight, begun, blocks)
    some = spread.shape[1]
    for i in range(size):
        spread[i] = act[:some, :]
    rest[...] = act[some:, :]


def last_b_kernel(size, distances, place, weight, begun, *refs):
    *blocks, rest, out = refs
    out[: rest.shape[0], :] = rest[...]
    out[rest.shape[0] :, :] = activation(size, distances, place, weight, begun, blocks)


def pack_kernel(first, second, third, fourth, out):
    rows = first.shape[0]
    for i, ref in enumerate((first, second, third)):
        out[i * rows : (i + 1) * rows, :] = ref[...]
    out[3 * rows :, :] = fourth[...]


def place_kernel(size, place, own, mine, other, out):
    rows = own.shape[0]
    me = place[0]

    def put(distance, value, start=0):
        at = lax.rem(me + distance, size)
        out[pl.ds(at, 1), start : start + value.shape[0], :] = value[None]

    def fill(a, b):
        put(1, b[0:rows, :])
        put(2, b[rows : 2 * rows, :])
        put(size - 3, b[2 * rows : 3 * rows, :])
        put(size - 1, a[0:rows, :])
        put(size - 2, a[rows : 2 * rows, :])
        put(3, a[2 * rows : 3 * rows, :])
        put(size // 2, a[3 * rows :, :])
        put(size // 2, b[3 * rows :, :], rows // 2)

    put(0, own[...])

    @pl.when(place[1] == 0)
    def _():
        fill(mine, other)

    @pl.when(place[1] == 1)
    def _():
        fill(other, mine)


def down_rows(down_weight, after, place, size, part, hidden):
    me, pair = lax.axis_index("tensor"), lax.axis_index("dp")
    blocks = down_weight.reshape(size, part, hidden)
    steps = ((1, 2, -3), (-1, -2, 3))
    got = []
    for first, second in zip(*steps):
        step = jnp.where(pair == 0, first, second)
        block = lax.dynamic_index_in_dim(blocks, lax.rem(me + step + size, size), 0, keepdims=False)
        perm = [(2 * i, 2 * ((i + first) % size)) for i in range(size)]
        perm += [(2 * i + 1, 2 * ((i + second) % size) + 1) for i in range(size)]
        got.append(lax.ppermute(block, ("tensor", "dp"), perm))
    half = part // 2
    far = lax.rem(me + size // 2, size)
    block = lax.dynamic_slice(blocks, (far, pair * half, 0), (1, half, hidden))[0]
    got.append(lax.ppermute(block, "tensor", shift(size, size // 2)))
    vmem = pl.BlockSpec(memory_space=pltpu.VMEM)
    mine = pl.pallas_call(
        pack_kernel,
        out_shape=jax.ShapeDtypeStruct((3 * part + half, hidden), blocks.dtype),
        in_specs=[vmem] * 4,
        out_specs=vmem,
        name="pack",
        compiler_params=SMALL,
    )(*got)
    other = lax.ppermute(mine, "dp", [(0, 1), (1, 0)])
    own = lax.dynamic_index_in_dim(blocks, me, 0, keepdims=False)
    placed = pl.pallas_call(
        functools.partial(place_kernel, size),
        out_shape=jax.ShapeDtypeStruct(blocks.shape, blocks.dtype),
        in_specs=[pl.BlockSpec(memory_space=pltpu.SMEM)] + [vmem] * 3,
        out_specs=vmem,
        name="place",
        compiler_params=SMALL,
    )(place, own, mine, other)
    return placed, after


def local(tokens, routes, gates, gate_up, down_weight, old_map, new_map):
    experts = lax.axis_size(EXPERT)
    size = lax.axis_size("tensor")
    me = lax.axis_index("tensor")
    tok_rows, part = tokens.shape
    picks = routes.shape[1]
    capacity = (tok_rows * picks + experts - 1) // experts
    hidden = down_weight.shape[2]
    rows = experts * capacity
    bf16 = jnp.bfloat16

    slot_ids = jnp.arange(experts, dtype=jnp.int32)
    holder = jnp.sum(jnp.where(new_map[:, None] == old_map[None, :], slot_ids[None, :], 0), axis=1)
    target = jnp.sum(
        jnp.where(routes[:, :, None] == slot_ids[None, None, :], holder[None, None, :], 0), axis=2
    )
    hits = target[:, :, None] == slot_ids[None, None, :]
    member = jnp.any(hits, axis=1)
    weight = jnp.sum(jnp.where(hits, gates[:, :, None], 0.0), axis=1)
    ones = jnp.tril(jnp.ones((tok_rows, tok_rows), bf16), -1)
    position = dot(ones, member.astype(bf16)).astype(jnp.int32)
    place = jnp.where(member, position, -1)
    cap_ids = jnp.arange(capacity, dtype=jnp.int32)
    matches = place[:, :, None] == cap_ids[None, None, :]
    assign = matches.astype(bf16).reshape(tok_rows, rows)
    combine = jnp.where(matches, weight[:, :, None], 0.0).reshape(tok_rows, rows)
    outgoing = dot(assign, tokens, ((0,), (0,))).astype(bf16)

    def exchange(x):
        x = x.reshape(experts, capacity // 2, 2, part)
        x = lax.all_to_all(x, EXPERT, 0, 0, tiled=True)
        return x.reshape(rows, part)

    arrived = lax.optimization_barrier(exchange(outgoing))
    place = jnp.stack([me, lax.axis_index("dp")]).astype(jnp.int32)
    down_mine, weight_in = down_rows(down_weight, gate_up, place, size, part, hidden)

    chains = [hops(arrived[: rows // 2], size, 1), hops(arrived[rows // 2 :], size, -1)]
    weight_in = pl.pallas_call(
        relayout_kernel,
        grid=(size,),
        out_shape=jax.ShapeDtypeStruct((size, part, 2 * hidden), bf16),
        in_specs=[pl.BlockSpec((1, part, 2, hidden), lambda i: (0, i, 0, 0))],
        out_specs=pl.BlockSpec((1, part, 2 * hidden), lambda i: (i, 0, 0)),
        name="relayout",
        compiler_params=SMALL,
    )(weight_in)
    early = 5
    smem, vmem = pl.BlockSpec(memory_space=pltpu.SMEM), pl.BlockSpec(memory_space=pltpu.VMEM)
    begun = pl.pallas_call(
        functools.partial(first_kernel, size, [d for d, _ in chains[0][:early]]),
        out_shape=[jax.ShapeDtypeStruct((rows // 2, 2 * hidden), jnp.float32)] * 2,
        in_specs=[smem] + [vmem] * (1 + 2 * early),
        out_specs=[vmem] * 2,
        name="first",
        compiler_params=SMALL,
    )(place, weight_in, *(x for chain in chains for _, x in chain[:early]))

    some = 80
    distances = [d for d, _ in chains[0][early:]]
    late = [smem] + [vmem] * (2 + len(distances))
    spread, rest = pl.pallas_call(
        functools.partial(last_a_kernel, size, distances),
        out_shape=[
            jax.ShapeDtypeStruct((size, some, hidden), bf16),
            jax.ShapeDtypeStruct((rows // 2 - some, hidden), bf16),
        ],
        in_specs=late,
        out_specs=[vmem] * 2,
        name="last_a",
        compiler_params=SMALL,
    )(place, weight_in, begun[0], *(x for _, x in chains[0][early:]))
    all_a = lax.all_to_all(spread, "tensor", 0, 0, tiled=True)
    act_b = pl.pallas_call(
        functools.partial(last_b_kernel, size, distances),
        out_shape=jax.ShapeDtypeStruct((rows - some, hidden), bf16),
        in_specs=late + [vmem],
        out_specs=vmem,
        name="last_b",
        compiler_params=SMALL,
    )(place, weight_in, begun[1], *(x for _, x in chains[1][early:]), rest)
    all_b = lax.all_gather(act_b, "tensor")

    def outputs(act):
        return dot(act, down_mine, ((0, 2), (0, 2))).astype(bf16)

    expert_out = jnp.concatenate([outputs(all_a), outputs(all_b)], axis=0)
    returned = exchange(expert_out)
    mixed = jnp.dot(
        combine,
        returned.astype(jnp.float32),
        precision=lax.Precision.HIGHEST,
        preferred_element_type=jnp.float32,
    )
    return mixed.astype(bf16)


def solution(mesh):
    split = Mesh(
        mesh.devices.reshape(4, 4, 2, mesh.shape["tensor"], mesh.shape["dp"]),
        ("expert_0", "expert_1", "expert_2", "tensor", "dp"),
    )
    in_specs = (
        P(DP_EXPERT, "tensor"),
        P(DP_EXPERT, None),
        P(DP_EXPERT, None),
        P(EXPERT, None, None, "tensor"),
        P(EXPERT, None, "tensor"),
        P(),
        P(),
    )
    return jax.shard_map(local, mesh=split, in_specs=in_specs, out_specs=P(DP_EXPERT, "tensor"), check_vma=False)
```

```python
import functools

import jax
import jax.numpy as jnp
from jax import lax
from jax.experimental import pallas as pl
from jax.experimental.pallas import tpu as pltpu
from jax.sharding import Mesh
from jax.sharding import PartitionSpec as P


EXPERT = ("expert_0", "expert_1", "expert_2")
SMALL = pltpu.CompilerParams(vmem_limit_bytes=12 * 1024 * 1024)
DP_EXPERT = ("dp", "expert_0", "expert_1", "expert_2")


def dot(a, b, dims=((1,), (0,))):
    return lax.dot_general(a, b, (dims, ((), ())), preferred_element_type=jnp.float32)


def shift(size, step):
    return [(i, (i + step) % size) for i in range(size)]


def hops(x, size):
    half = x.shape[0] // 2
    up = lax.ppermute(x, "tensor", shift(size, 1))
    down = lax.ppermute(x, "tensor", shift(size, -1))
    near = [(0, x), (-1, up), (1, down)]
    ups, downs, far = [up[:half], up[half:]], [down[:half], down[half:]], [[], []]
    for step in range(2, size // 2):
        for i in range(2):
            ups[i] = lax.ppermute(ups[i], "tensor", shift(size, 1))
            downs[i] = lax.ppermute(downs[i], "tensor", shift(size, -1))
            far[i] += [(-step, ups[i]), (step, downs[i])]
    far[0].append((size // 2, lax.ppermute(ups[0], "tensor", shift(size, 1))))
    far[1].append((size // 2, lax.ppermute(downs[1], "tensor", shift(size, -1))))
    return near, far


def relayout_kernel(x, out):
    out[0] = x[0].reshape(out.shape[1:])


def product_of(me, size, distances, blocks, weight):
    return sum(
        jnp.dot(x[...], weight[lax.rem(me + d + size, size)], preferred_element_type=jnp.float32)
        for d, x in zip(distances, blocks)
    )


def first_kernel(size, near, far, place, weight, *refs):
    half = refs[-1].shape[0]
    for chain in range(2):
        blocks = [x.at[chain * half : (chain + 1) * half] for x in refs[: len(near)]]
        start = len(near) + chain * len(far)
        blocks += refs[start : start + len(far)]
        refs[chain - 2][...] = product_of(place[0], size, near + far, blocks, weight)


def activation(size, distances, place, weight, begun, blocks):
    total = begun[...] + product_of(place[0], size, distances, blocks, weight)
    gate, up = total[:, : total.shape[1] // 2], total[:, total.shape[1] // 2 :]
    return (gate / (1.0 + jnp.exp(-gate)) * up).astype(jnp.bfloat16)


def last_a_kernel(size, distances, place, weight, begun, *refs):
    *blocks, spread, rest = refs
    act = activation(size, distances, place, weight, begun, blocks)
    some = spread.shape[1]
    for i in range(size):
        spread[i] = act[:some, :]
    rest[...] = act[some:, :]


def last_b_kernel(size, distances, place, weight, begun, *refs):
    *blocks, rest, out = refs
    out[: rest.shape[0], :] = rest[...]
    out[rest.shape[0] :, :] = activation(size, distances, place, weight, begun, blocks)


def pack_kernel(first, second, third, fourth, out):
    rows = first.shape[0]
    for i, ref in enumerate((first, second, third)):
        out[i * rows : (i + 1) * rows, :] = ref[...]
    out[3 * rows :, :] = fourth[...]


def place_kernel(size, place, own, mine, other, out):
    rows = own.shape[0]
    me = place[0]

    def put(distance, value, start=0):
        at = lax.rem(me + distance, size)
        out[pl.ds(at, 1), start : start + value.shape[0], :] = value[None]

    def fill(a, b):
        put(1, b[0:rows, :])
        put(2, b[rows : 2 * rows, :])
        put(size - 3, b[2 * rows : 3 * rows, :])
        put(size - 1, a[0:rows, :])
        put(size - 2, a[rows : 2 * rows, :])
        put(3, a[2 * rows : 3 * rows, :])
        put(size // 2, a[3 * rows :, :])
        put(size // 2, b[3 * rows :, :], rows // 2)

    put(0, own[...])

    @pl.when(place[1] == 0)
    def _():
        fill(mine, other)

    @pl.when(place[1] == 1)
    def _():
        fill(other, mine)


def down_rows(down_weight, after, place, size, part, hidden):
    me, pair = lax.axis_index("tensor"), lax.axis_index("dp")
    blocks = down_weight.reshape(size, part, hidden)
    steps = ((1, 2, -3), (-1, -2, 3))
    got = []
    for first, second in zip(*steps):
        step = jnp.where(pair == 0, first, second)
        block = lax.dynamic_index_in_dim(blocks, lax.rem(me + step + size, size), 0, keepdims=False)
        perm = [(2 * i, 2 * ((i + first) % size)) for i in range(size)]
        perm += [(2 * i + 1, 2 * ((i + second) % size) + 1) for i in range(size)]
        got.append(lax.ppermute(block, ("tensor", "dp"), perm))
    half = part // 2
    far = lax.rem(me + size // 2, size)
    block = lax.dynamic_slice(blocks, (far, pair * half, 0), (1, half, hidden))[0]
    got.append(lax.ppermute(block, "tensor", shift(size, size // 2)))
    vmem = pl.BlockSpec(memory_space=pltpu.VMEM)
    mine = pl.pallas_call(
        pack_kernel,
        out_shape=jax.ShapeDtypeStruct((3 * part + half, hidden), blocks.dtype),
        in_specs=[vmem] * 4,
        out_specs=vmem,
        name="pack",
        compiler_params=SMALL,
    )(*got)
    other = lax.ppermute(mine, "dp", [(0, 1), (1, 0)])
    own = lax.dynamic_index_in_dim(blocks, me, 0, keepdims=False)
    placed = pl.pallas_call(
        functools.partial(place_kernel, size),
        out_shape=jax.ShapeDtypeStruct(blocks.shape, blocks.dtype),
        in_specs=[pl.BlockSpec(memory_space=pltpu.SMEM)] + [vmem] * 3,
        out_specs=vmem,
        name="place",
        compiler_params=SMALL,
    )(place, own, mine, other)
    return placed, after


def local(tokens, routes, gates, gate_up, down_weight, old_map, new_map):
    experts = lax.axis_size(EXPERT)
    size = lax.axis_size("tensor")
    me = lax.axis_index("tensor")
    tok_rows, part = tokens.shape
    picks = routes.shape[1]
    capacity = (tok_rows * picks + experts - 1) // experts
    hidden = down_weight.shape[2]
    rows = experts * capacity
    bf16 = jnp.bfloat16

    slot_ids = jnp.arange(experts, dtype=jnp.int32)
    holder = jnp.sum(jnp.where(new_map[:, None] == old_map[None, :], slot_ids[None, :], 0), axis=1)
    target = jnp.sum(
        jnp.where(routes[:, :, None] == slot_ids[None, None, :], holder[None, None, :], 0), axis=2
    )
    hits = target[:, :, None] == slot_ids[None, None, :]
    member = jnp.any(hits, axis=1)
    weight = jnp.sum(jnp.where(hits, gates[:, :, None], 0.0), axis=1)
    ones = jnp.tril(jnp.ones((tok_rows, tok_rows), bf16), -1)
    position = dot(ones, member.astype(bf16)).astype(jnp.int32)
    place = jnp.where(member, position, -1)
    cap_ids = jnp.arange(capacity, dtype=jnp.int32)
    matches = place[:, :, None] == cap_ids[None, None, :]
    assign = matches.astype(bf16).reshape(tok_rows, rows)
    combine = jnp.where(matches, weight[:, :, None], 0.0).reshape(tok_rows, rows)
    outgoing = dot(assign, tokens, ((0,), (0,))).astype(bf16)

    def exchange(x):
        x = x.reshape(experts, capacity // 2, 2, part)
        x = lax.all_to_all(x, EXPERT, 0, 0, tiled=True)
        return x.reshape(rows, part)

    arrived = lax.optimization_barrier(exchange(outgoing))
    place = jnp.stack([me, lax.axis_index("dp")]).astype(jnp.int32)
    down_mine, weight_in = down_rows(down_weight, gate_up, place, size, part, hidden)

    near, far = hops(arrived, size)
    weight_in = pl.pallas_call(
        relayout_kernel,
        grid=(size,),
        out_shape=jax.ShapeDtypeStruct((size, part, 2 * hidden), bf16),
        in_specs=[pl.BlockSpec((1, part, 2, hidden), lambda i: (0, i, 0, 0))],
        out_specs=pl.BlockSpec((1, part, 2 * hidden), lambda i: (i, 0, 0)),
        name="relayout",
        compiler_params=SMALL,
    )(weight_in)
    early = 2
    smem, vmem = pl.BlockSpec(memory_space=pltpu.SMEM), pl.BlockSpec(memory_space=pltpu.VMEM)
    begun = pl.pallas_call(
        functools.partial(first_kernel, size, [d for d, _ in near], [d for d, _ in far[0][:early]]),
        out_shape=[jax.ShapeDtypeStruct((rows // 2, 2 * hidden), jnp.float32)] * 2,
        in_specs=[smem] + [vmem] * (1 + len(near) + 2 * early),
        out_specs=[vmem] * 2,
        name="first",
        compiler_params=SMALL,
    )(place, weight_in, *(x for _, x in near), *(x for chain in far for _, x in chain[:early]))

    some = 80
    distances = [d for d, _ in far[0][early:]]
    late = [smem] + [vmem] * (2 + len(distances))
    spread, rest = pl.pallas_call(
        functools.partial(last_a_kernel, size, distances),
        out_shape=[
            jax.ShapeDtypeStruct((size, some, hidden), bf16),
            jax.ShapeDtypeStruct((rows // 2 - some, hidden), bf16),
        ],
        in_specs=late,
        out_specs=[vmem] * 2,
        name="last_a",
        compiler_params=SMALL,
    )(place, weight_in, begun[0], *(x for _, x in far[0][early:]))
    all_a = lax.all_to_all(spread, "tensor", 0, 0, tiled=True)
    act_b = pl.pallas_call(
        functools.partial(last_b_kernel, size, distances),
        out_shape=jax.ShapeDtypeStruct((rows - some, hidden), bf16),
        in_specs=late + [vmem],
        out_specs=vmem,
        name="last_b",
        compiler_params=SMALL,
    )(place, weight_in, begun[1], *(x for _, x in far[1][early:]), rest)
    all_b = lax.all_gather(act_b, "tensor")

    def outputs(act):
        return dot(act, down_mine, ((0, 2), (0, 2))).astype(bf16)

    expert_out = jnp.concatenate([outputs(all_a), outputs(all_b)], axis=0)
    returned = exchange(expert_out)
    mixed = jnp.dot(
        combine,
        returned.astype(jnp.float32),
        precision=lax.Precision.HIGHEST,
        preferred_element_type=jnp.float32,
    )
    return mixed.astype(bf16)


def solution(mesh):
    split = Mesh(
        mesh.devices.reshape(4, 4, 2, mesh.shape["tensor"], mesh.shape["dp"]),
        ("expert_0", "expert_1", "expert_2", "tensor", "dp"),
    )
    in_specs = (
        P(DP_EXPERT, "tensor"),
        P(DP_EXPERT, None),
        P(DP_EXPERT, None),
        P(EXPERT, None, None, "tensor"),
        P(EXPERT, None, "tensor"),
        P(),
        P(),
    )
    return jax.shard_map(local, mesh=split, in_specs=in_specs, out_specs=P(DP_EXPERT, "tensor"), check_vma=False)
```

```python
import functools

import jax
import jax.numpy as jnp
from jax import lax
from jax.experimental import pallas as pl
from jax.experimental.pallas import tpu as pltpu
from jax.sharding import Mesh
from jax.sharding import PartitionSpec as P


EXPERT = ("expert_0", "expert_1", "expert_2")
SMALL = pltpu.CompilerParams(vmem_limit_bytes=12 * 1024 * 1024)
DP_EXPERT = ("dp", "expert_0", "expert_1", "expert_2")


def dot(a, b, dims=((1,), (0,))):
    return lax.dot_general(a, b, (dims, ((), ())), preferred_element_type=jnp.float32)


def shift(size, step):
    return [(i, (i + step) % size) for i in range(size)]


def hops(x, size, last):
    found = [(0, x)]
    up = down = x
    for step in range(1, size // 2):
        up = lax.ppermute(up, "tensor", shift(size, 1))
        down = lax.ppermute(down, "tensor", shift(size, -1))
        found += [(-step, up), (step, down)]
    found.append((size // 2, lax.ppermute(up if last > 0 else down, "tensor", shift(size, last))))
    return found


def relayout_kernel(x, out):
    out[0] = x[0].reshape(out.shape[1:])


def product_of(me, size, distances, blocks, weight):
    return sum(
        jnp.dot(x[...], weight[lax.rem(me + d + size, size)], preferred_element_type=jnp.float32)
        for d, x in zip(distances, blocks)
    )


def first_kernel(size, distances, place, weight, *refs):
    count = len(distances)
    for chain in range(2):
        blocks = refs[chain * count : (chain + 1) * count]
        refs[2 * count + chain][...] = product_of(place[0], size, distances, blocks, weight)


def activation(size, distances, place, weight, begun, blocks):
    total = begun[...] + product_of(place[0], size, distances, blocks, weight)
    gate, up = total[:, : total.shape[1] // 2], total[:, total.shape[1] // 2 :]
    return (gate / (1.0 + jnp.exp(-gate)) * up).astype(jnp.bfloat16)


def last_a_kernel(size, distances, place, weight, begun, *refs):
    *blocks, spread, rest = refs
    act = activation(size, distances, place, weight, begun, blocks)
    some = spread.shape[1]
    for i in range(size):
        spread[i] = act[:some, :]
    rest[...] = act[some:, :]


def last_b_kernel(size, distances, place, weight, begun, *refs):
    *blocks, rest, out = refs
    out[: rest.shape[0], :] = rest[...]
    out[rest.shape[0] :, :] = activation(size, distances, place, weight, begun, blocks)


def route_kernel(capacity, routes, old_map, new_map, tokens, out, place):
    picks, count = routes.shape
    experts = old_map.shape[1]
    rows = experts * capacity
    bf16 = jnp.bfloat16

    def ids(shape, axis):
        return lax.broadcasted_iota(jnp.int32, shape, axis)

    def ones(hit):
        return jnp.where(hit, 1.0, 0.0).astype(bf16)

    named = routes[...]
    slots = ids((experts, count), 0)
    chosen = sum(jnp.where(named[k : k + 1, :] == slots, 1.0, 0.0) for k in range(picks)).astype(bf16)
    values = ids((experts, experts), 0)
    chosen = dot(ones(values == new_map[...]), chosen).astype(bf16)
    chosen = dot(ones(values == old_map[...]), chosen, ((0,), (0,)))
    before = ones(ids((count, count), 0) < ids((count, count), 1))
    position = jnp.where(chosen > 0.5, dot(chosen.astype(bf16), before), -1.0)
    place[...] = position.astype(jnp.int32)
    row = ids((rows, experts), 0) - capacity * ids((rows, experts), 1)
    inside = (row >= 0) & (row < capacity)
    wanted = jnp.sum(jnp.where(inside, row, 0).astype(jnp.float32), axis=1, keepdims=True)
    assign = ones(dot(ones(inside), position.astype(bf16)) == wanted)
    out[...] = dot(assign, tokens[...]).astype(out.dtype)


def pack_kernel(first, second, third, fourth, out):
    rows = first.shape[0]
    for i, ref in enumerate((first, second, third)):
        out[i * rows : (i + 1) * rows, :] = ref[...]
    out[3 * rows :, :] = fourth[...]


def place_kernel(size, place, own, mine, other, out):
    rows = own.shape[0]
    me = place[0]

    def put(distance, value, start=0):
        at = lax.rem(me + distance, size)
        out[pl.ds(at, 1), start : start + value.shape[0], :] = value[None]

    def fill(a, b):
        put(1, b[0:rows, :])
        put(2, b[rows : 2 * rows, :])
        put(size - 3, b[2 * rows : 3 * rows, :])
        put(size - 1, a[0:rows, :])
        put(size - 2, a[rows : 2 * rows, :])
        put(3, a[2 * rows : 3 * rows, :])
        put(size // 2, a[3 * rows :, :])
        put(size // 2, b[3 * rows :, :], rows // 2)

    put(0, own[...])

    @pl.when(place[1] == 0)
    def _():
        fill(mine, other)

    @pl.when(place[1] == 1)
    def _():
        fill(other, mine)


def down_rows(down_weight, after, place, size, part, hidden):
    me, pair = lax.axis_index("tensor"), lax.axis_index("dp")
    blocks = down_weight.reshape(size, part, hidden)
    steps = ((1, 2, -3), (-1, -2, 3))
    got = []
    for first, second in zip(*steps):
        step = jnp.where(pair == 0, first, second)
        block = lax.dynamic_index_in_dim(blocks, lax.rem(me + step + size, size), 0, keepdims=False)
        perm = [(2 * i, 2 * ((i + first) % size)) for i in range(size)]
        perm += [(2 * i + 1, 2 * ((i + second) % size) + 1) for i in range(size)]
        got.append(lax.ppermute(block, ("tensor", "dp"), perm))
    half = part // 2
    far = lax.rem(me + size // 2, size)
    block = lax.dynamic_slice(blocks, (far, pair * half, 0), (1, half, hidden))[0]
    got.append(lax.ppermute(block, "tensor", shift(size, size // 2)))
    vmem = pl.BlockSpec(memory_space=pltpu.VMEM)
    mine = pl.pallas_call(
        pack_kernel,
        out_shape=jax.ShapeDtypeStruct((3 * part + half, hidden), blocks.dtype),
        in_specs=[vmem] * 4,
        out_specs=vmem,
        name="pack",
        compiler_params=SMALL,
    )(*got)
    other = lax.ppermute(mine, "dp", [(0, 1), (1, 0)])
    own = lax.dynamic_index_in_dim(blocks, me, 0, keepdims=False)
    placed = pl.pallas_call(
        functools.partial(place_kernel, size),
        out_shape=jax.ShapeDtypeStruct(blocks.shape, blocks.dtype),
        in_specs=[pl.BlockSpec(memory_space=pltpu.SMEM)] + [vmem] * 3,
        out_specs=vmem,
        name="place",
        compiler_params=SMALL,
    )(place, own, mine, other)
    return placed, after


def local(tokens, routes, gates, gate_up, down_weight, old_map, new_map):
    experts = lax.axis_size(EXPERT)
    size = lax.axis_size("tensor")
    me = lax.axis_index("tensor")
    tok_rows, part = tokens.shape
    picks = routes.shape[1]
    capacity = (tok_rows * picks + experts - 1) // experts
    hidden = down_weight.shape[2]
    rows = experts * capacity
    bf16 = jnp.bfloat16

    vmem = pl.BlockSpec(memory_space=pltpu.VMEM)
    outgoing, position = pl.pallas_call(
        functools.partial(route_kernel, capacity),
        out_shape=[
            jax.ShapeDtypeStruct((rows, part), bf16),
            jax.ShapeDtypeStruct((experts, tok_rows), jnp.int32),
        ],
        in_specs=[vmem] * 4,
        out_specs=[vmem] * 2,
        name="route",
        compiler_params=SMALL,
    )(routes.T, old_map.reshape(1, experts), new_map.reshape(1, experts), tokens)

    def exchange(x):
        x = x.reshape(experts, capacity // 2, 2, part)
        x = lax.all_to_all(x, EXPERT, 0, 0, tiled=True)
        return x.reshape(rows, part)

    arrived = lax.optimization_barrier(exchange(outgoing))
    place = jnp.stack([me, lax.axis_index("dp")]).astype(jnp.int32)
    down_mine, weight_in = down_rows(down_weight, gate_up, place, size, part, hidden)

    chains = [hops(arrived[: rows // 2], size, 1), hops(arrived[rows // 2 :], size, -1)]
    weight_in = pl.pallas_call(
        relayout_kernel,
        grid=(size,),
        out_shape=jax.ShapeDtypeStruct((size, part, 2 * hidden), bf16),
        in_specs=[pl.BlockSpec((1, part, 2, hidden), lambda i: (0, i, 0, 0))],
        out_specs=pl.BlockSpec((1, part, 2 * hidden), lambda i: (i, 0, 0)),
        name="relayout",
        compiler_params=SMALL,
    )(weight_in)
    early = 5
    smem = pl.BlockSpec(memory_space=pltpu.SMEM)
    begun = pl.pallas_call(
        functools.partial(first_kernel, size, [d for d, _ in chains[0][:early]]),
        out_shape=[jax.ShapeDtypeStruct((rows // 2, 2 * hidden), jnp.float32)] * 2,
        in_specs=[smem] + [vmem] * (1 + 2 * early),
        out_specs=[vmem] * 2,
        name="first",
        compiler_params=SMALL,
    )(place, weight_in, *(x for chain in chains for _, x in chain[:early]))

    some = 80
    distances = [d for d, _ in chains[0][early:]]
    late = [smem] + [vmem] * (2 + len(distances))
    spread, rest = pl.pallas_call(
        functools.partial(last_a_kernel, size, distances),
        out_shape=[
            jax.ShapeDtypeStruct((size, some, hidden), bf16),
            jax.ShapeDtypeStruct((rows // 2 - some, hidden), bf16),
        ],
        in_specs=late,
        out_specs=[vmem] * 2,
        name="last_a",
        compiler_params=SMALL,
    )(place, weight_in, begun[0], *(x for _, x in chains[0][early:]))
    all_a = lax.all_to_all(spread, "tensor", 0, 0, tiled=True)
    act_b = pl.pallas_call(
        functools.partial(last_b_kernel, size, distances),
        out_shape=jax.ShapeDtypeStruct((rows - some, hidden), bf16),
        in_specs=late + [vmem],
        out_specs=vmem,
        name="last_b",
        compiler_params=SMALL,
    )(place, weight_in, begun[1], *(x for _, x in chains[1][early:]), rest)
    all_b = lax.all_gather(act_b, "tensor")

    def outputs(act):
        return dot(act, down_mine, ((0, 2), (0, 2))).astype(bf16)

    expert_out = jnp.concatenate([outputs(all_a), outputs(all_b)], axis=0)
    expert_out, routes, gates, position, old_map, new_map = lax.optimization_barrier(
        (expert_out, routes, gates, position, old_map, new_map)
    )
    returned = exchange(expert_out)
    slot_ids = jnp.arange(experts, dtype=jnp.int32)
    holder = jnp.sum(jnp.where(new_map[:, None] == old_map[None, :], slot_ids[None, :], 0), axis=1)
    target = jnp.sum(
        jnp.where(routes[:, :, None] == slot_ids[None, None, :], holder[None, None, :], 0), axis=2
    )
    hits = target[:, :, None] == slot_ids[None, None, :]
    weight = jnp.sum(jnp.where(hits, gates[:, :, None], 0.0), axis=1)
    matches = position.T[:, :, None] == jnp.arange(capacity, dtype=jnp.int32)[None, None, :]
    combine = jnp.where(matches, weight[:, :, None], 0.0).reshape(tok_rows, rows)
    mixed = jnp.dot(
        combine,
        returned.astype(jnp.float32),
        precision=lax.Precision.HIGHEST,
        preferred_element_type=jnp.float32,
    )
    return mixed.astype(bf16)


def solution(mesh):
    split = Mesh(
        mesh.devices.reshape(4, 4, 2, mesh.shape["tensor"], mesh.shape["dp"]),
        ("expert_0", "expert_1", "expert_2", "tensor", "dp"),
    )
    in_specs = (
        P(DP_EXPERT, "tensor"),
        P(DP_EXPERT, None),
        P(DP_EXPERT, None),
        P(EXPERT, None, None, "tensor"),
        P(EXPERT, None, "tensor"),
        P(),
        P(),
    )
    return jax.shard_map(local, mesh=split, in_specs=in_specs, out_specs=P(DP_EXPERT, "tensor"), check_vma=False)
```
